128 devices in a mesh: grp: 2 (over y_lo), seq: 32 (over x, z, core), dp: 2 (over y_hi).
Axes of the slice: x: 4, y: 4 (y_hi: 2, y_lo: 2; y = y_hi * 2 + y_lo), z: 4, core: 2. Of those that a mesh axis runs over, the one named last changes fastest.
Arguments:
- counts: int32 [2, 32, 2, 256, 1024], P('dp', 'seq', 'grp'), may hold values from 0 to 23
- valid_frames: int32 [2, 4], replicated, may hold values from 2 to 16, as said below
- cotangent: bfloat16 [2, 64, 256, 1024], P('dp', 'seq'), may hold values from -0.125 to 0.125
- pillar_proj: bfloat16 [1024, 1024], replicated, may hold values from -0.1875 to 0.1875
- pillar_gain: float32 [1024], replicated, may hold values from 0.1 to 1.9
- latent_proj: bfloat16 [1024, 1024], replicated, may hold values from -0.1875 to 0.1875
- input_proj: bfloat16 [1024, 1024], replicated, may hold values from -0.1875 to 0.1875
- space_gain: float32 [1024], replicated, may hold values from 0.1 to 1.9
- space_project: bfloat16 [1024, 3072], replicated, may hold values from -0.1875 to 0.1875
- space_output: bfloat16 [1024, 1024], replicated, may hold values from -0.1875 to 0.1875
- time_gain: float32 [1024], replicated, may hold values from 0.1 to 1.9
- time_project: bfloat16 [1024, 3072], replicated, may hold values from -0.1875 to 0.1875
- time_output: bfloat16 [1024, 1024], replicated, may hold values from -0.75 to 0.75
Outputs:
- pillar_grad: float32 [1024, 1024], P(('grp', 'seq', 'dp'))
- latent_grad: float32 [1024, 1024], P(('grp', 'seq', 'dp'))
The draws below stay inside these ranges and needn't reach their ends.
Inputs may be any that keep to these rules, and one draw needn't show every extreme that they name: `valid_frames`: exactly one scene has all 16 frames valid.
All inputs are finite; a program needn't handle non-finite values.
Results may differ from the reference program's by a relative error of at most 0.0095.
Values may be sent and summed in bfloat16 or wider, within the bound.
No kernel may reach another device: no remote copies, remote signals or barrier semaphores. Data moves between devices by JAX's collectives and lax.ppermute only.
A program may use at most 128 MiB of HBM per device.

```python
import math
import jax
import jax.numpy as jnp
import numpy as np
from jax import lax

LAT = 1024
D = 1024
HEADS = 8
INNER = 1024
PIN = 1024
HT = 1024
FRAMES = 16
P_SIZE = 256
SCN = 4
SFG = 64
PAIRS = 32
GROUPS = 2


def draw_valid_frames(key, part):
    total = GROUPS * SCN
    drawn = jax.random.randint(jax.random.fold_in(key, 11), (total,), 2, FRAMES)
    full_index = jax.random.randint(jax.random.fold_in(key, 12), (), 0, total)
    drawn = jnp.where(jnp.arange(total) == full_index, FRAMES, drawn)
    return drawn.reshape(GROUPS, SCN).astype(jnp.int32)


def set_ends(result, stream_key, least, top_value):
    longest = result.shape.index(max(result.shape))
    spots = []
    for shift in (0, 1):
        where = [jax.random.randint(jax.random.fold_in(stream_key, axis), (), 0, length) for axis, length in enumerate(result.shape)]
        where[longest] = (where[longest] + shift) % result.shape[longest]
        spots.append(tuple(where))
    return result.at[spots[0]].set(least).at[spots[1]].set(top_value)


def block_scale(stream_key, dims, pieces, low, high):
    level, own = 1.0, jax.random.fold_in(stream_key, 6)
    for dim, parts in pieces:
        heights = jnp.exp(jax.random.uniform(jax.random.fold_in(own, dim), (parts,), jnp.float32, low / len(pieces), high / len(pieces)))
        level = level * jnp.repeat(heights, dims[dim] // parts).reshape([-1 if axis == dim else 1 for axis in range(len(dims))])
    return level


def cumulative_ranks(amount, lean):
    loads = [(1 << 20) // math.isqrt(rank ** lean) + 1 for rank in range(1, amount + 1)]
    width = 1 + sum(loads) // (1 << 30)
    return np.cumsum(np.array([max(1, weight // width) for weight in loads]))


def ranked_ids(stream_key, shape, amount, slope):
    table = cumulative_ranks(amount, slope)
    ticket = jax.random.randint(jax.random.fold_in(stream_key, 1), shape, 0, int(table[amount - 1]))
    grade = jnp.searchsorted(jnp.asarray(table, jnp.int32), ticket, side="right")
    return jax.random.permutation(jax.random.fold_in(stream_key, 2), amount)[grade].astype(jnp.int32)


def gaussian(key, extent, deviation, reach, shards=(), kind=jnp.bfloat16):
    entries = deviation * jax.random.normal(key, extent, jnp.float32)
    if shards:
        entries = entries * block_scale(key, extent, shards, -0.22, 0.18)
    return jnp.clip(entries, -reach, reach).astype(kind)


def setup_inputs(seed: int = 0) -> dict:
    seeds = jax.random.split(jax.random.key(seed), 14)
    return {
        "counts": set_ends(ranked_ids(seeds[0], (GROUPS, PAIRS, 2, P_SIZE, PIN), 24, 2), jax.random.fold_in(seeds[0], 3), 0, 23).astype(jnp.int32),
        "valid_frames": draw_valid_frames(jax.random.fold_in(seeds[13], 71), 0),
        "cotangent": gaussian(seeds[2], (GROUPS, SFG, P_SIZE, D), 0.02, 0.125, ((0, 2), (1, 32))),
        "pillar_proj": gaussian(seeds[3], (PIN, HT), PIN ** -0.5, 0.1875),
        "pillar_gain": jnp.clip(1.0 + 0.18 * jax.random.normal(seeds[4], (HT,), jnp.float32), 0.1, 1.9),
        "latent_proj": gaussian(seeds[5], (HT, LAT), HT ** -0.5, 0.1875),
        "input_proj": gaussian(seeds[6], (LAT, D), LAT ** -0.5, 0.1875),
        "space_gain": jnp.clip(1.0 + 0.18 * jax.random.normal(seeds[7], (D,), jnp.float32), 0.1, 1.9),
        "space_project": gaussian(seeds[8], (D, 3 * INNER), D ** -0.5, 0.1875),
        "space_output": gaussian(seeds[9], (INNER, D), INNER ** -0.5, 0.1875),
        "time_gain": jnp.clip(1.0 + 0.18 * jax.random.normal(seeds[10], (D,), jnp.float32), 0.1, 1.9),
        "time_project": gaussian(seeds[11], (D, 3 * INNER), D ** -0.5, 0.1875),
        "time_output": gaussian(seeds[12], (INNER, D), (INNER // 16) ** -0.5, 0.75),
    }


def scaled_norm(values, norm_gain):
    return values * lax.rsqrt(lax.optimization_barrier(jnp.mean(values * values, axis=-1, keepdims=True)) + 1e-06) * norm_gain

def head_norm(values):
    values = values.astype(jnp.float32)
    return (values * lax.rsqrt(lax.optimization_barrier(jnp.mean(values * values, axis=-1, keepdims=True)) + 1e-06)).astype(jnp.bfloat16)

def project(activations, weight):
    return jnp.dot(activations, weight, preferred_element_type=jnp.float32)

def split_heads(joined, head_count):
    shaped = joined.reshape(joined.shape[:-1] + (3, head_count, joined.shape[-1] // (3 * head_count)))
    return (head_norm(shaped[..., 0, :, :]), head_norm(shaped[..., 1, :, :]), shaped[..., 2, :, :])

def space_core(joined, head_count):
    queries, keys, values = split_heads(joined, head_count)
    score_scale = queries.shape[-1] ** (-0.5)
    scores = jnp.einsum('grphd,grqhd->grhpq', queries.astype(jnp.float32), keys.astype(jnp.float32)) * score_scale
    weights = jnp.exp(scores)
    weights = (weights / lax.optimization_barrier(jnp.sum(weights, axis=-1, keepdims=True))).astype(jnp.bfloat16)
    mixture = jnp.einsum('grhpq,grqhd->grphd', weights.astype(jnp.float32), values.astype(jnp.float32))
    return mixture.astype(jnp.bfloat16).reshape(joined.shape[:-1] + (-1,))

def time_core(joined, head_count, visible):
    queries, keys, values = split_heads(joined, head_count)
    score_scale = queries.shape[-1] ** (-0.5)
    scores = jnp.einsum('gsfthd,gsethd->gsthfe', queries.astype(jnp.float32), keys.astype(jnp.float32)) * score_scale
    weights = jnp.exp(scores) * visible
    weights = (weights / lax.optimization_barrier(jnp.sum(weights, axis=-1, keepdims=True))).astype(jnp.bfloat16)
    mixture = jnp.einsum('gsthfe,gsethd->gsfthd', weights.astype(jnp.float32), values.astype(jnp.float32))
    return mixture.astype(jnp.bfloat16).reshape(joined.shape[:-1] + (-1,))

def mixer_inputs(residual, norm_gain, weight):
    return project(scaled_norm(residual, norm_gain).astype(jnp.bfloat16), weight).astype(jnp.bfloat16)

def space_layer(stream, norm_gain, weight_in, weight_out, head_count):
    residual = stream.astype(jnp.float32)
    joined = mixer_inputs(residual, norm_gain, weight_in)
    return (residual + project(space_core(joined, head_count), weight_out)).astype(jnp.bfloat16)

def time_layer(stream, norm_gain, weight_in, weight_out, head_count, visible):
    residual = stream.astype(jnp.float32)
    joined = mixer_inputs(residual, norm_gain, weight_in)
    return residual + project(time_core(joined, head_count, visible), weight_out)

def visibility(valid_rows, frame_count):
    position = jnp.arange(frame_count, dtype=jnp.int32)
    causal = position[None, :] <= position[:, None]
    allowed = causal[None, None] & (position[None, None, None, :] < valid_rows[:, :, None, None])
    return allowed.astype(jnp.float32)[:, :, None, None]

def activation(inputs, norm_gain):
    return jax.nn.gelu(scaled_norm(inputs, norm_gain))

def reference(counts, valid_frames, cotangent, pillar_proj, pillar_gain, latent_proj, input_proj, space_gain, space_project, space_output, time_gain, time_project, time_output):
    features = jnp.log1p(counts.astype(jnp.float32)).astype(jnp.bfloat16)
    before = project(features, pillar_proj)
    hidden, activation_back = jax.vjp(lambda inputs: activation(inputs, pillar_gain), before)
    hidden = hidden.astype(jnp.bfloat16)
    latents = project(hidden, latent_proj).astype(jnp.bfloat16).reshape(GROUPS, SFG, P_SIZE, LAT)
    visible = visibility(valid_frames, FRAMES)

    def single_frame(stream):
        return space_layer(stream, space_gain, space_project, space_output, HEADS)

    def world(latent_in):
        stream = project(latent_in, input_proj).astype(jnp.bfloat16)
        framed = lax.map(single_frame, stream.reshape(GROUPS * SFG, 1, 1, P_SIZE, D))
        return time_layer(framed.reshape(GROUPS, SCN, FRAMES, P_SIZE, D), time_gain, time_project, time_output, HEADS, visible)
    unused, world_back = jax.vjp(world, latents)
    stream_grad = world_back(cotangent.reshape(GROUPS, SCN, FRAMES, P_SIZE, D).astype(jnp.float32))[0]
    token_grad = stream_grad.reshape(GROUPS, PAIRS, 2, P_SIZE, LAT)
    hidden_grad = jnp.einsum('abcpl,hl->abcph', token_grad.astype(jnp.float32), latent_proj.astype(jnp.float32))
    before_grad = activation_back(hidden_grad)[0].astype(jnp.bfloat16)
    latent_sum = jnp.einsum('th,tl->hl', hidden.reshape(-1, HT).astype(jnp.float32), token_grad.reshape(-1, LAT).astype(jnp.float32))
    pillar_sum = jnp.einsum('tp,th->ph', features.reshape(-1, PIN).astype(jnp.float32), before_grad.reshape(-1, HT).astype(jnp.float32))
    return (pillar_sum, latent_sum)
```

```python
import jax
import jax.numpy as jnp
from jax import lax
from jax.experimental import pallas as pl
from jax.experimental.pallas import tpu as pltpu
from jax.sharding import Mesh, PartitionSpec as P

HEADS = 8
HEAD = 128
FRAMES = 16
TOK = 256
D = 1024
EPS = 1e-06
F32 = jnp.float32
BF16 = jnp.bfloat16
SCALE = HEAD**-0.5
VMEM = pl.BlockSpec(memory_space=pltpu.VMEM)
SMEM = pl.BlockSpec(memory_space=pltpu.SMEM)
ANY = pl.BlockSpec(memory_space=pl.ANY)


def dot(a, b):
    return lax.dot_general(a, b, (((1,), (0,)), ((), ())), preferred_element_type=F32)


def dot_nt(a, b):
    return lax.dot_general(a, b, (((1,), (1,)), ((), ())), preferred_element_type=F32)


def dot_tn(a, b):
    return lax.dot_general(a, b, (((0,), (0,)), ((), ())), preferred_element_type=F32)


def inverse_rms(values):
    return lax.rsqrt(jnp.mean(values * values, axis=-1, keepdims=True) + EPS)


def norm_back(values, inverse, grad):
    inner = jnp.mean(values * grad, axis=-1, keepdims=True)
    return inverse * grad - values * (inverse * inverse * inverse * inner)


GELU_A = 0.7978845608028654
GELU_B = 0.044715


def fetch(pairs, sems):
    copies = [
        pltpu.make_async_copy(src, dst, sems.at[k]) for k, (src, dst) in enumerate(pairs)
    ]
    for copy in copies:
        copy.start()
    return copies


def head_parts(j_ref, h):
    q = j_ref[:, pl.ds(pl.multiple_of(h * HEAD, HEAD), HEAD)].astype(F32)
    k = j_ref[:, pl.ds(pl.multiple_of(D + h * HEAD, HEAD), HEAD)].astype(F32)
    v = j_ref[:, pl.ds(pl.multiple_of(2 * D + h * HEAD, HEAD), HEAD)]
    iq = inverse_rms(q)
    ik = inverse_rms(k)
    return q, k, v, iq, ik, (q * iq).astype(BF16), (k * ik).astype(BF16)


def softmax(qn, kn, mask):
    w = jnp.exp(dot_nt(qn, kn) * SCALE)
    if mask is not None:
        w = w * mask
    return w / jnp.sum(w, axis=-1, keepdims=True)


def attention_back(j_ref, dm_ref, dj_ref, mask, h):
    q, k, v, iq, ik, qn, kn = head_parts(j_ref, h)
    weights = softmax(qn, kn, mask)
    cols = pl.ds(pl.multiple_of(h * HEAD, HEAD), HEAD)
    dm = dm_ref[:, cols]
    dp = dot_nt(dm, v).astype(BF16).astype(F32)
    dv = dot_tn(weights.astype(BF16), dm)
    ds = weights * (dp - jnp.sum(dp * weights, axis=-1, keepdims=True)) * SCALE
    ds = ds.astype(BF16)
    dqn = dot(ds, kn).astype(BF16).astype(F32)
    dkn = dot_tn(ds, qn).astype(BF16).astype(F32)
    dj_ref[:, cols] = norm_back(q, iq, dqn).astype(BF16)
    dj_ref[:, pl.ds(pl.multiple_of(D + h * HEAD, HEAD), HEAD)] = norm_back(k, ik, dkn).astype(BF16)
    dj_ref[:, pl.ds(pl.multiple_of(2 * D + h * HEAD, HEAD), HEAD)] = dv.astype(BF16)


def front_kernel(
    counts, pillar_proj, pillar_gain, latent_proj, input_proj, space_gain, space_project,
    space_output, features, before, hidden, stream, joined, spaced,
    w_pillar, w_latent, w_input, w_project, w_output, mixed, sems,
):
    copies = fetch(
        [
            (pillar_proj, w_pillar),
            (latent_proj, w_latent),
            (input_proj, w_input),
            (space_project, w_project),
            (space_output, w_output),
        ],
        sems,
    )
    x = jnp.log(counts[...].astype(F32) + 1.0).astype(BF16)
    features[...] = x
    copies[0].wait()
    b = dot(x, w_pillar[...])
    before[...] = b
    n = b * inverse_rms(b) * pillar_gain[...]
    hid = (0.5 * n * (1.0 + jnp.tanh(GELU_A * (n + GELU_B * n * n * n)))).astype(BF16)
    hidden[...] = hid
    copies[1].wait()
    lat = dot(hid, w_latent[...]).astype(BF16)
    copies[2].wait()
    s = dot(lat, w_input[...]).astype(BF16)
    stream[...] = s
    s = s.astype(F32)
    u = (s * inverse_rms(s) * space_gain[...]).astype(BF16)
    copies[3].wait()
    for part in range(3):
        cols = slice(part * D, (part + 1) * D)
        joined[:, cols] = dot(u, w_project[:, cols]).astype(BF16)

    def head(h, carry):
        q, k, v, iq, ik, qn, kn = head_parts(joined, h)
        weights = softmax(qn, kn, None).astype(BF16)
        mixed[:, pl.ds(pl.multiple_of(h * HEAD, HEAD), HEAD)] = dot(weights, v).astype(BF16)
        return carry

    lax.fori_loop(0, HEADS, head, 0)
    copies[4].wait()
    spaced[...] = (stream[...].astype(F32) + dot(mixed[...], w_output[...])).astype(BF16)


def turn_kernel(features, hidden, feat_own, feat_send, hid_own, hid_send, turned):
    core = lax.axis_index("core")
    for src, own, send in ((features, feat_own, feat_send), (hidden, hid_own, hid_send)):
        turned[...] = src[...].T.reshape(32, 2, 16, TOK)
        own[...] = turned[:, core].reshape(512, TOK)
        send[...] = turned[:, 1 - core].reshape(512, TOK)


def mixture_kernel(cot, time_output, out):
    out[...] = dot_nt(cot[...], time_output[...]).astype(BF16)


def time_kernel(
    valid_frames, spaced, cot, dmixed, time_gain, time_project, grad,
    w_project, joined, djoined, masked, sems,
):
    copies = fetch([(time_project, w_project)], sems)
    valid = valid_frames[lax.axis_index("dp"), lax.axis_index("x")]
    row = lax.broadcasted_iota(jnp.int32, (TOK, TOK), 0)
    col = lax.broadcasted_iota(jnp.int32, (TOK, TOK), 1)
    e = col // FRAMES
    seen = (row % FRAMES == col % FRAMES) & (e <= row // FRAMES) & (e < valid)
    masked[...] = seen.astype(F32)
    s = spaced[...].astype(F32)
    inverse = inverse_rms(s)
    u = (s * inverse * time_gain[...]).astype(BF16)
    copies[0].wait()
    for part in range(3):
        cols = slice(part * D, (part + 1) * D)
        joined[:, cols] = dot(u, w_project[:, cols]).astype(BF16)

    def head(h, carry):
        attention_back(joined, dmixed, djoined, masked[...], h)
        return carry

    lax.fori_loop(0, HEADS, head, 0)
    du = dot_nt(djoined[...], w_project[...]).astype(BF16).astype(F32) * time_gain[...]
    s = spaced[...].astype(F32)
    grad[...] = (cot[...].astype(F32) + norm_back(s, inverse_rms(s), du)).astype(BF16)


def back_kernel(
    dspaced, joined, stream, space_gain, space_output, space_project, input_proj, dlatent,
    w_output, w_project, w_input, dmixed, djoined, sems,
):
    copies = fetch(
        [(space_output, w_output), (space_project, w_project), (input_proj, w_input)], sems
    )
    copies[0].wait()
    dmixed[...] = dot_nt(dspaced[...], w_output[...]).astype(BF16)

    def head(h, carry):
        attention_back(joined, dmixed, djoined, None, h)
        return carry

    lax.fori_loop(0, HEADS, head, 0)
    copies[1].wait()
    du = dot_nt(djoined[...], w_project[...]).astype(BF16).astype(F32) * space_gain[...]
    s = stream[...].astype(F32)
    dstream = (dspaced[...].astype(F32) + norm_back(s, inverse_rms(s), du)).astype(BF16)
    copies[2].wait()
    dlatent[...] = dot_nt(dstream, w_input[...]).astype(BF16)


def token_kernel(dlatent, before, pillar_gain, latent_proj, dbefore):
    dhid = dot_nt(dlatent[...], latent_proj[...])
    b = before[...]
    inverse = inverse_rms(b)
    n = b * inverse * pillar_gain[...]
    t = jnp.tanh(GELU_A * (n + GELU_B * n * n * n))
    slope = 0.5 * (1.0 + t) + 0.5 * n * (1.0 - t * t) * (GELU_A * (1.0 + 3.0 * GELU_B * n * n))
    dn = dhid * slope * pillar_gain[...]
    dbefore[...] = norm_back(b, inverse, dn).astype(BF16)


def weight_kernel(own, other, grad_own, grad_other, out):
    out[...] = (dot(own[...], grad_own[...]) + dot(other[...], grad_other[...])).astype(BF16)


def total_kernel(a, b, out_a, out_b):
    for src, out in ((a, out_a), (b, out_b)):
        out[...] = jnp.sum(src[...].astype(F32).reshape(64, 8, D), axis=0)


def struct(shape, dtype):
    return jax.ShapeDtypeStruct(shape, dtype)


def call(kernel, name, outs, in_specs, args, scratch=(), flops=0, bytes_accessed=0, limit=None):
    many = isinstance(outs, tuple)
    return pl.pallas_call(
        kernel,
        out_shape=outs,
        in_specs=in_specs,
        out_specs=tuple(VMEM for _ in outs) if many else VMEM,
        scratch_shapes=list(scratch),
        name=name,
        cost_estimate=pl.CostEstimate(
            flops=flops, bytes_accessed=bytes_accessed, transcendentals=0
        ),
        compiler_params=pltpu.CompilerParams(vmem_limit_bytes=limit),
    )(*args)


UNIT = 2 * TOK * D * D
MIB = 1 << 20


def shards(
    counts,
    valid_frames,
    cotangent,
    pillar_proj,
    pillar_gain,
    latent_proj,
    input_proj,
    space_gain,
    space_project,
    space_output,
    time_gain,
    time_project,
    time_output,
):
    rows = struct((TOK, D), BF16)
    scene = ("z", "core", "grp")
    rest = ("grp", "x", "z", "dp")
    swap = ((0, 1), (1, 0))
    pillar_gain = pillar_gain.reshape(1, D)
    space_gain = space_gain.reshape(1, D)
    time_gain = time_gain.reshape(1, D)

    def exchange(values, axes):
        return lax.all_to_all(values, axes, split_axis=0, concat_axis=0, tiled=True)

    own_cot = lax.dynamic_index_in_dim(cotangent[0], lax.axis_index("grp"), 0, keepdims=False)
    cot = exchange(own_cot, scene)

    wide = lambda n: pltpu.VMEM((D, n * D), BF16)
    features, before, hidden, stream, joined, spaced = call(
        front_kernel,
        "front",
        (rows, struct((TOK, D), F32), rows, rows, struct((TOK, 3 * D), BF16), rows),
        [VMEM, ANY, VMEM, ANY, ANY, VMEM, ANY, ANY],
        (
            counts.reshape(TOK, D), pillar_proj, pillar_gain, latent_proj, input_proj,
            space_gain, space_project, space_output,
        ),
        [wide(1), wide(1), wide(1), wide(3), wide(1), pltpu.VMEM((TOK, D), BF16),
         pltpu.SemaphoreType.DMA((5,))],
        8 * UNIT,
        20 * MIB,
    )
    half = struct((512, TOK), BF16)
    spaced_tok = exchange(spaced, scene)
    feat_own, feat_send, hid_own, hid_send = call(
        turn_kernel,
        "turn",
        (half, half, half, half),
        [VMEM, VMEM],
        (features, hidden),
        [pltpu.VMEM((32, 2, 16, TOK), BF16)],
        0,
        2 * MIB,
    )
    feat_other = lax.ppermute(feat_send, "core", swap)
    hid_other = lax.ppermute(hid_send, "core", swap)
    dmixed = call(mixture_kernel, "mixture", rows, [VMEM, VMEM], (cot, time_output), (), UNIT, 3 * MIB)
    grad_tok = call(
        time_kernel,
        "time",
        rows,
        [SMEM, VMEM, VMEM, VMEM, VMEM, ANY],
        (valid_frames, spaced_tok, cot, dmixed, time_gain, time_project),
        [wide(3), pltpu.VMEM((TOK, 3 * D), BF16), pltpu.VMEM((TOK, 3 * D), BF16),
         pltpu.VMEM((TOK, TOK), F32), pltpu.SemaphoreType.DMA((1,))],
        8 * UNIT,
        10 * MIB,
    )
    dspaced = exchange(grad_tok, scene)
    dlatent = call(
        back_kernel,
        "back",
        rows,
        [VMEM, VMEM, VMEM, VMEM, ANY, ANY, ANY],
        (dspaced, joined, stream, space_gain, space_output, space_project, input_proj),
        [wide(1), wide(3), wide(1), pltpu.VMEM((TOK, D), BF16), pltpu.VMEM((TOK, 3 * D), BF16),
         pltpu.SemaphoreType.DMA((3,))],
        7 * UNIT,
        14 * MIB,
    )
    dlatent_other = lax.ppermute(dlatent, "core", swap)
    dbefore = call(
        token_kernel,
        "token",
        rows,
        [VMEM, VMEM, VMEM, VMEM],
        (dlatent, before, pillar_gain, latent_proj),
        (),
        UNIT,
        4 * MIB,
    )
    dbefore_other = lax.ppermute(dbefore, "core", swap)
    partial = struct((512, D), BF16)
    latent_part = call(
        weight_kernel, "latent_weight", partial, [VMEM] * 4,
        (hid_own, hid_other, dlatent, dlatent_other), (), UNIT, 2 * MIB,
    )
    latent_parts = exchange(latent_part, rest)
    pillar_part = call(
        weight_kernel, "pillar_weight", partial, [VMEM] * 4,
        (feat_own, feat_other, dbefore, dbefore_other), (), UNIT, 2 * MIB,
    )
    pillar_parts = exchange(pillar_part, rest)
    out = struct((8, D), F32)
    return call(total_kernel, "total", (out, out), [VMEM, VMEM], (pillar_parts, latent_parts), (), 0, 2 * MIB)


def solution(mesh):
    split = Mesh(mesh.devices.reshape(2, 4, 4, 2, 2), ("grp", "x", "z", "core", "dp"))
    seq = ("x", "z", "core")
    placed = (P("dp", seq, "grp", None, None), P(), P("dp", seq, None, None)) + (P(),) * 10
    out = P(("grp", "x", "z", "core", "dp"), None)
    return jax.shard_map(
        shards, mesh=split, in_specs=placed, out_specs=(out, out), check_vma=False
    )
```

```python
import jax
import jax.numpy as jnp
from jax import lax
from jax.experimental import pallas as pl
from jax.experimental.pallas import tpu as pltpu
from jax.sharding import Mesh, PartitionSpec as P

HEADS = 8
HEAD = 128
FRAMES = 16
TOK = 256
D = 1024
EPS = 1e-06
F32 = jnp.float32
BF16 = jnp.bfloat16
SCALE = HEAD**-0.5
VMEM = pl.BlockSpec(memory_space=pltpu.VMEM)
SMEM = pl.BlockSpec(memory_space=pltpu.SMEM)
HBM = pl.BlockSpec(memory_space=pltpu.HBM)


def dot(a, b):
    return lax.dot_general(a, b, (((1,), (0,)), ((), ())), preferred_element_type=F32)


def dot_nt(a, b):
    return lax.dot_general(a, b, (((1,), (1,)), ((), ())), preferred_element_type=F32)


def dot_tn(a, b):
    return lax.dot_general(a, b, (((0,), (0,)), ((), ())), preferred_element_type=F32)


def inverse_rms(values):
    return lax.rsqrt(jnp.mean(values * values, axis=-1, keepdims=True) + EPS)


def norm_back(values, inverse, grad):
    inner = jnp.mean(values * grad, axis=-1, keepdims=True)
    return inverse * grad - values * (inverse * inverse * inverse * inner)


GELU_A = 0.7978845608028654
GELU_B = 0.044715


def fetch(pairs, sems):
    copies = [
        pltpu.make_async_copy(src, dst, sems.at[k]) for k, (src, dst) in enumerate(pairs)
    ]
    for copy in copies:
        copy.start()
    return copies


def head_parts(j_ref, h):
    q = j_ref[:, pl.ds(pl.multiple_of(h * HEAD, HEAD), HEAD)].astype(F32)
    k = j_ref[:, pl.ds(pl.multiple_of(D + h * HEAD, HEAD), HEAD)].astype(F32)
    v = j_ref[:, pl.ds(pl.multiple_of(2 * D + h * HEAD, HEAD), HEAD)]
    iq = inverse_rms(q)
    ik = inverse_rms(k)
    return q, k, v, iq, ik, (q * iq).astype(BF16), (k * ik).astype(BF16)


def softmax(qn, kn, mask):
    w = jnp.exp(dot_nt(qn, kn) * SCALE)
    if mask is not None:
        w = w * mask
    return w / jnp.sum(w, axis=-1, keepdims=True)


def attention_back(j_ref, dm_ref, dj_ref, mask, h):
    q, k, v, iq, ik, qn, kn = head_parts(j_ref, h)
    weights = softmax(qn, kn, mask)
    cols = pl.ds(pl.multiple_of(h * HEAD, HEAD), HEAD)
    dm = dm_ref[:, cols]
    dp = dot_nt(dm, v).astype(BF16).astype(F32)
    dv = dot_tn(weights.astype(BF16), dm)
    ds = weights * (dp - jnp.sum(dp * weights, axis=-1, keepdims=True)) * SCALE
    ds = ds.astype(BF16)
    dqn = dot(ds, kn).astype(BF16).astype(F32)
    dkn = dot_tn(ds, qn).astype(BF16).astype(F32)
    dj_ref[:, cols] = norm_back(q, iq, dqn).astype(BF16)
    dj_ref[:, pl.ds(pl.multiple_of(D + h * HEAD, HEAD), HEAD)] = norm_back(k, ik, dkn).astype(BF16)
    dj_ref[:, pl.ds(pl.multiple_of(2 * D + h * HEAD, HEAD), HEAD)] = dv.astype(BF16)


def front_kernel(
    counts, cotangent, pillar_proj, pillar_gain, latent_proj, input_proj, space_gain,
    space_project, space_output, features, before, hidden, stream, joined, packed,
    w_pillar, w_latent, w_input, w_project, w_output, counted, mixed,
    v_features, v_before, v_hidden, v_stream, v_joined, sems, out_sems,
):
    copies = fetch(
        [
            (counts, counted),
            (pillar_proj, w_pillar),
            (latent_proj, w_latent),
            (input_proj, w_input),
            (space_project, w_project),
            (space_output, w_output),
            (cotangent.at[lax.axis_index("grp")], packed.at[:, 1]),
        ],
        sems,
    )
    saves = [
        pltpu.make_async_copy(src, dst, out_sems.at[k])
        for k, (src, dst) in enumerate(
            (
                (v_features, features),
                (v_before, before),
                (v_hidden, hidden),
                (v_stream, stream),
                (v_joined, joined),
            )
        )
    ]
    copies[0].wait()
    x = jnp.log(counted[...].astype(F32) + 1.0).astype(BF16)
    v_features[...] = x
    saves[0].start()
    copies[1].wait()
    b = dot(x, w_pillar[...])
    v_before[...] = b
    saves[1].start()
    n = b * inverse_rms(b) * pillar_gain[...]
    hid = (0.5 * n * (1.0 + jnp.tanh(GELU_A * (n + GELU_B * n * n * n)))).astype(BF16)
    v_hidden[...] = hid
    saves[2].start()
    copies[2].wait()
    lat = dot(hid, w_latent[...]).astype(BF16)
    copies[3].wait()
    s = dot(lat, w_input[...]).astype(BF16)
    v_stream[...] = s
    saves[3].start()
    s = s.astype(F32)
    u = (s * inverse_rms(s) * space_gain[...]).astype(BF16)
    copies[4].wait()
    for part in range(3):
        cols = slice(part * D, (part + 1) * D)
        v_joined[:, cols] = dot(u, w_project[:, cols]).astype(BF16)
    saves[4].start()

    def head(h, carry):
        q, k, v, iq, ik, qn, kn = head_parts(v_joined, h)
        weights = softmax(qn, kn, None).astype(BF16)
        mixed[:, pl.ds(pl.multiple_of(h * HEAD, HEAD), HEAD)] = dot(weights, v).astype(BF16)
        return carry

    lax.fori_loop(0, HEADS, head, 0, unroll=True)
    copies[5].wait()
    spaced = (v_stream[...].astype(F32) + dot(mixed[...], w_output[...])).astype(BF16)
    packed[:, 0] = spaced.reshape(16, 16, D)
    copies[6].wait()
    for save in saves:
        save.wait()


def turn_kernel(features, hidden, feat_own, feat_send, hid_own, hid_send, turned):
    core = lax.axis_index("core")
    for src, own, send in ((features, feat_own, feat_send), (hidden, hid_own, hid_send)):
        turned[...] = src[...].T.reshape(32, 2, 16, TOK)
        own[...] = turned[:, core].reshape(512, TOK)
        send[...] = turned[:, 1 - core].reshape(512, TOK)


def time_kernel(
    valid_frames, packed, time_gain, w_project, w_output, grad, joined, dmixed, djoined, masked
):
    valid = valid_frames[lax.axis_index("dp"), lax.axis_index("x")]
    row = lax.broadcasted_iota(jnp.int32, (TOK, TOK), 0)
    col = lax.broadcasted_iota(jnp.int32, (TOK, TOK), 1)
    e = col // FRAMES
    seen = (row % FRAMES == col % FRAMES) & (e <= row // FRAMES) & (e < valid)
    masked[...] = seen.astype(F32)
    cot = packed[:, 1].reshape(TOK, D)
    dmixed[...] = dot_nt(cot, w_output[...]).astype(BF16)
    s = packed[:, 0].reshape(TOK, D).astype(F32)
    inverse = inverse_rms(s)
    u = (s * inverse * time_gain[...]).astype(BF16)
    for part in range(3):
        cols = slice(part * D, (part + 1) * D)
        joined[:, cols] = dot(u, w_project[:, cols]).astype(BF16)

    def head(h, carry):
        attention_back(joined, dmixed, djoined, masked[...], h)
        return carry

    lax.fori_loop(0, HEADS, head, 0, unroll=True)
    du = dot_nt(djoined[...], w_project[...]).astype(BF16).astype(F32) * time_gain[...]
    s = packed[:, 0].reshape(TOK, D).astype(F32)
    cot = packed[:, 1].reshape(TOK, D).astype(F32)
    grad[...] = (cot + norm_back(s, inverse_rms(s), du)).astype(BF16)


def back_kernel(
    dspaced, joined, stream, space_gain, w_output, w_project, w_input, dlatent, dmixed, djoined
):
    dmixed[...] = dot_nt(dspaced[...], w_output[...]).astype(BF16)

    def head(h, carry):
        attention_back(joined, dmixed, djoined, None, h)
        return carry

    lax.fori_loop(0, HEADS, head, 0, unroll=True)
    du = dot_nt(djoined[...], w_project[...]).astype(BF16).astype(F32) * space_gain[...]
    s = stream[...].astype(F32)
    dstream = (dspaced[...].astype(F32) + norm_back(s, inverse_rms(s), du)).astype(BF16)
    dlatent[...] = dot_nt(dstream, w_input[...]).astype(BF16)


def token_kernel(dlatent, before, pillar_gain, latent_proj, dbefore):
    dhid = dot_nt(dlatent[...], latent_proj[...])
    b = before[...]
    inverse = inverse_rms(b)
    n = b * inverse * pillar_gain[...]
    t = jnp.tanh(GELU_A * (n + GELU_B * n * n * n))
    slope = 0.5 * (1.0 + t) + 0.5 * n * (1.0 - t * t) * (GELU_A * (1.0 + 3.0 * GELU_B * n * n))
    dn = dhid * slope * pillar_gain[...]
    dbefore[...] = norm_back(b, inverse, dn).astype(BF16)


def latent_kernel(own, other, grad_own, grad_other, out):
    out[...] = (dot(own[...], grad_own[...]) + dot(other[...], grad_other[...])).astype(BF16)


def pillar_kernel(own, other, grad_own, grad_other, latent, out):
    part = dot(own[...], grad_own[...]) + dot(other[...], grad_other[...])
    out[:, 0] = part.reshape(64, 8, D).astype(BF16)
    out[:, 1] = latent[...].reshape(64, 8, D)


def total_kernel(parts, pillar, latent):
    for k, out in ((0, pillar), (1, latent)):
        out[...] = jnp.sum(parts[:, k].astype(F32), axis=0)


def struct(shape, dtype):
    return jax.ShapeDtypeStruct(shape, dtype)


def call(kernel, name, outs, in_specs, args, scratch=(), flops=0, bytes_accessed=0, limit=28 << 20, out_specs=None):
    many = isinstance(outs, tuple)
    return pl.pallas_call(
        kernel,
        out_shape=outs,
        in_specs=in_specs,
        out_specs=out_specs or (tuple(VMEM for _ in outs) if many else VMEM),
        scratch_shapes=list(scratch),
        name=name,
        cost_estimate=pl.CostEstimate(
            flops=flops, bytes_accessed=bytes_accessed, transcendentals=0
        ),
        compiler_params=pltpu.CompilerParams(vmem_limit_bytes=limit),
    )(*args)


UNIT = 2 * TOK * D * D
MIB = 1 << 20


def shards(
    counts,
    valid_frames,
    cotangent,
    pillar_proj,
    pillar_gain,
    latent_proj,
    input_proj,
    space_gain,
    space_project,
    space_output,
    time_gain,
    time_project,
    time_output,
):
    rows = struct((TOK, D), BF16)
    scene = ("z", "core", "grp")
    swap = ((0, 1), (1, 0))
    pillar_gain = pillar_gain.reshape(1, D)
    space_gain = space_gain.reshape(1, D)
    time_gain = time_gain.reshape(1, D)

    def exchange(values, axes):
        return lax.all_to_all(values, axes, split_axis=0, concat_axis=0, tiled=True)

    wide = lambda n, dtype=BF16: pltpu.VMEM((D, n * D), dtype)
    tall = lambda n, dtype=BF16: pltpu.VMEM((TOK, n * D), dtype)
    features, before, hidden, stream, joined, packed = call(
        front_kernel,
        "front",
        (rows, struct((TOK, D), F32), rows, rows, struct((TOK, 3 * D), BF16),
         struct((16, 2, 16, D), BF16)),
        [HBM, HBM, HBM, VMEM, HBM, HBM, VMEM, HBM, HBM],
        (
            counts.reshape(TOK, D), cotangent.reshape(2, 16, 16, D), pillar_proj, pillar_gain,
            latent_proj, input_proj, space_gain, space_project, space_output,
        ),
        [wide(1), wide(1), wide(1), wide(3), wide(1), tall(1, jnp.int32), tall(1),
         tall(1), tall(1, F32), tall(1), tall(1), tall(3),
         pltpu.SemaphoreType.DMA((7,)), pltpu.SemaphoreType.DMA((5,))],
        8 * UNIT,
        20 * MIB,
        None,
        [HBM, HBM, HBM, HBM, HBM, VMEM],
    )
    packed = exchange(packed, scene)
    half = struct((512, TOK), BF16)
    feat_own, feat_send, hid_own, hid_send = call(
        turn_kernel,
        "turn",
        (half, half, half, half),
        [VMEM, VMEM],
        (features, hidden),
        [pltpu.VMEM((32, 2, 16, TOK), BF16)],
        0,
        2 * MIB,
    )
    feat_other = lax.ppermute(feat_send, "core", swap)
    hid_other = lax.ppermute(hid_send, "core", swap)
    grad_tok = call(
        time_kernel,
        "time",
        rows,
        [SMEM, VMEM, VMEM, VMEM, VMEM],
        (valid_frames, packed, time_gain, time_project, time_output),
        [tall(3), tall(1), tall(3), pltpu.VMEM((TOK, TOK), F32)],
        9 * UNIT,
        10 * MIB,
    )
    dspaced = exchange(grad_tok, scene)
    dlatent = call(
        back_kernel,
        "back",
        rows,
        [VMEM] * 7,
        (dspaced, joined, stream, space_gain, space_output, space_project, input_proj),
        [tall(1), tall(3)],
        7 * UNIT,
        14 * MIB,
    )
    dlatent_other = lax.ppermute(dlatent, "core", swap)
    dbefore = call(
        token_kernel,
        "token",
        rows,
        [VMEM, VMEM, VMEM, VMEM],
        (dlatent, before, pillar_gain, latent_proj),
        (),
        UNIT,
        4 * MIB,
    )
    dbefore_other = lax.ppermute(dbefore, "core", swap)
    latent_part = call(
        latent_kernel, "latent_weight", struct((512, D), BF16), [VMEM] * 4,
        (hid_own, hid_other, dlatent, dlatent_other), (), UNIT, 2 * MIB,
    )
    parts = call(
        pillar_kernel, "pillar_weight", struct((64, 2, 8, D), BF16), [VMEM] * 5,
        (feat_own, feat_other, dbefore, dbefore_other, latent_part), (), UNIT, 4 * MIB,
    )
    parts = exchange(parts, ("grp", "x", "z", "dp"))
    out = struct((8, D), F32)
    return call(total_kernel, "total", (out, out), [VMEM], (parts,), (), 0, 2 * MIB)


def solution(mesh):
    split = Mesh(mesh.devices.reshape(2, 4, 4, 2, 2), ("grp", "x", "z", "core", "dp"))
    seq = ("x", "z", "core")
    placed = (P("dp", seq, "grp", None, None), P(), P("dp", seq, None, None)) + (P(),) * 10
    out = P(("grp", "x", "z", "core", "dp"), None)
    return jax.shard_map(
        shards, mesh=split, in_specs=placed, out_specs=(out, out), check_vma=False
    )
```

```python
import jax
import jax.numpy as jnp
from jax import lax
from jax.experimental import pallas as pl
from jax.experimental.pallas import tpu as pltpu
from jax.sharding import Mesh, PartitionSpec as P

HEADS = 8
HEAD = 128
FRAMES = 16
TOK = 256
D = 1024
EPS = 1e-06
F32 = jnp.float32
BF16 = jnp.bfloat16
SCALE = HEAD**-0.5
VMEM = pl.BlockSpec(memory_space=pltpu.VMEM)
SMEM = pl.BlockSpec(memory_space=pltpu.SMEM)
HBM = pl.BlockSpec(memory_space=pltpu.HBM)


def dot(a, b):
    return lax.dot_general(a, b, (((1,), (0,)), ((), ())), preferred_element_type=F32)


def dot_nt(a, b):
    return lax.dot_general(a, b, (((1,), (1,)), ((), ())), preferred_element_type=F32)


def dot_tn(a, b):
    return lax.dot_general(a, b, (((0,), (0,)), ((), ())), preferred_element_type=F32)


def inverse_rms(values):
    return lax.rsqrt(jnp.mean(values * values, axis=-1, keepdims=True) + EPS)


def norm_back(values, inverse, grad):
    inner = jnp.mean(values * grad, axis=-1, keepdims=True)
    return inverse * grad - values * (inverse * inverse * inverse * inner)


GELU_A = 0.7978845608028654
GELU_B = 0.044715


def head_parts(j_ref, h):
    q = j_ref[:, pl.ds(pl.multiple_of(h * HEAD, HEAD), HEAD)].astype(F32)
    k = j_ref[:, pl.ds(pl.multiple_of(D + h * HEAD, HEAD), HEAD)].astype(F32)
    v = j_ref[:, pl.ds(pl.multiple_of(2 * D + h * HEAD, HEAD), HEAD)]
    iq = inverse_rms(q)
    ik = inverse_rms(k)
    return q, k, v, iq, ik, (q * iq).astype(BF16), (k * ik).astype(BF16)


def softmax(qn, kn, mask):
    w = jnp.exp(dot_nt(qn, kn) * SCALE)
    if mask is not None:
        w = w * mask
    return w / jnp.sum(w, axis=-1, keepdims=True)


def attention_back(j_ref, dm_ref, dj_ref, mask, h):
    q, k, v, iq, ik, qn, kn = head_parts(j_ref, h)
    weights = softmax(qn, kn, mask)
    cols = pl.ds(pl.multiple_of(h * HEAD, HEAD), HEAD)
    dm = dm_ref[:, cols]
    dp = dot_nt(dm, v).astype(BF16).astype(F32)
    dv = dot_tn(weights.astype(BF16), dm)
    ds = weights * (dp - jnp.sum(dp * weights, axis=-1, keepdims=True)) * SCALE
    ds = ds.astype(BF16)
    dqn = dot(ds, kn).astype(BF16).astype(F32)
    dkn = dot_tn(ds, qn).astype(BF16).astype(F32)
    dj_ref[:, cols] = norm_back(q, iq, dqn).astype(BF16)
    dj_ref[:, pl.ds(pl.multiple_of(D + h * HEAD, HEAD), HEAD)] = norm_back(k, ik, dkn).astype(BF16)
    dj_ref[:, pl.ds(pl.multiple_of(2 * D + h * HEAD, HEAD), HEAD)] = dv.astype(BF16)


def front_kernel(
    counts, cotangent, pillar_proj, pillar_gain, latent_proj, input_proj, space_gain,
    space_project, space_output, own, send, before, stream, joined, packed,
    w_pillar, w_latent, w_input, w_project, w_output, counted, mixed,
    v_turned, v_before, v_stream, v_joined, sems, out_sems,
):
    core = lax.axis_index("core")
    copies = [
        pltpu.make_async_copy(src, dst, sems.at[k])
        for k, (src, dst) in enumerate(
            (
                (counts, counted),
                (pillar_proj, w_pillar),
                (latent_proj, w_latent),
                (input_proj, w_input),
                (space_project.at[:, pl.ds(0, D)], w_project.at[:, pl.ds(0, D)]),
                (space_output, w_output),
                (cotangent.at[lax.axis_index("grp")], packed.at[:, 1]),
                (space_project.at[:, pl.ds(D, D)], w_project.at[:, pl.ds(D, D)]),
                (space_project.at[:, pl.ds(2 * D, D)], w_project.at[:, pl.ds(2 * D, D)]),
            )
        )
    ]
    saves = [
        pltpu.make_async_copy(src, dst, out_sems.at[k])
        for k, (src, dst) in enumerate(
            (
                (v_turned.at[:, core], own),
                (v_turned.at[:, 1 - core], send),
                (v_before, before),
                (v_stream, stream),
                (v_joined, joined),
            )
        )
    ]

    def turn(values, k):
        blocks = values.T.reshape(32, 2, 16, TOK)
        v_turned[k, 0] = blocks[:, 0].reshape(512, TOK)
        v_turned[k, 1] = blocks[:, 1].reshape(512, TOK)

    for k in (0, 1, 2, 3, 4, 7, 8, 5, 6):
        copies[k].start()
    copies[0].wait()
    x = jnp.log(counted[...].astype(F32) + 1.0).astype(BF16)
    copies[1].wait()
    b = dot(x, w_pillar[...])
    turn(x, 0)
    v_before[...] = b
    saves[2].start()
    n = b * inverse_rms(b) * pillar_gain[...]
    hid = (0.5 * n * (1.0 + jnp.tanh(GELU_A * (n + GELU_B * n * n * n)))).astype(BF16)
    copies[2].wait()
    lat = dot(hid, w_latent[...]).astype(BF16)
    turn(hid, 1)
    saves[0].start()
    saves[1].start()
    copies[3].wait()
    s = dot(lat, w_input[...]).astype(BF16)
    v_stream[...] = s
    saves[3].start()
    s = s.astype(F32)
    u = (s * inverse_rms(s) * space_gain[...]).astype(BF16)
    for part, k in enumerate((4, 7, 8)):
        copies[k].wait()
        cols = slice(part * D, (part + 1) * D)
        v_joined[:, cols] = dot(u, w_project[:, cols]).astype(BF16)
    saves[4].start()

    def head(h, carry):
        q, k, v, iq, ik, qn, kn = head_parts(v_joined, h)
        weights = softmax(qn, kn, None).astype(BF16)
        mixed[:, pl.ds(pl.multiple_of(h * HEAD, HEAD), HEAD)] = dot(weights, v).astype(BF16)
        return carry

    lax.fori_loop(0, HEADS, head, 0, unroll=True)
    copies[5].wait()
    spaced = (v_stream[...].astype(F32) + dot(mixed[...], w_output[...])).astype(BF16)
    packed[:, 0] = spaced.reshape(16, 16, D)
    copies[6].wait()
    for save in saves:
        save.wait()


def time_kernel(
    valid_frames, packed, time_gain, w_project, w_output, grad, joined, dmixed, djoined, masked
):
    valid = valid_frames[lax.axis_index("dp"), lax.axis_index("x")]
    row = lax.broadcasted_iota(jnp.int32, (TOK, TOK), 0)
    col = lax.broadcasted_iota(jnp.int32, (TOK, TOK), 1)
    e = col // FRAMES
    seen = (row % FRAMES == col % FRAMES) & (e <= row // FRAMES) & (e < valid)
    masked[...] = seen.astype(F32)
    s = packed[:, 0].reshape(TOK, D).astype(F32)
    inverse = inverse_rms(s)
    u = (s * inverse * time_gain[...]).astype(BF16)
    for part in range(3):
        cols = slice(part * D, (part + 1) * D)
        joined[:, cols] = dot(u, w_project[:, cols]).astype(BF16)
    dmixed[...] = dot_nt(packed[:, 1].reshape(TOK, D), w_output[...]).astype(BF16)

    def head(h, carry):
        attention_back(joined, dmixed, djoined, masked[...], h)
        return carry

    lax.fori_loop(0, HEADS, head, 0, unroll=True)
    du = dot_nt(djoined[...], w_project[...]).astype(BF16).astype(F32) * time_gain[...]
    s = packed[:, 0].reshape(TOK, D).astype(F32)
    cot = packed[:, 1].reshape(TOK, D).astype(F32)
    grad[...] = (cot + norm_back(s, inverse_rms(s), du)).astype(BF16)


def back_kernel(
    dspaced, joined, stream, space_gain, w_output, w_project, w_input, dlatent, dmixed, djoined
):
    dmixed[...] = dot_nt(dspaced[...], w_output[...]).astype(BF16)

    def head(h, carry):
        attention_back(joined, dmixed, djoined, None, h)
        return carry

    lax.fori_loop(0, HEADS, head, 0, unroll=True)
    du = dot_nt(djoined[...], w_project[...]).astype(BF16).astype(F32) * space_gain[...]
    s = stream[...].astype(F32)
    dstream = (dspaced[...].astype(F32) + norm_back(s, inverse_rms(s), du)).astype(BF16)
    dlatent[...] = dot_nt(dstream, w_input[...]).astype(BF16)


def token_kernel(dlatent, before, pillar_gain, latent_proj, dbefore):
    dhid = dot_nt(dlatent[...], latent_proj[...])
    b = before[...]
    inverse = inverse_rms(b)
    n = b * inverse * pillar_gain[...]
    t = jnp.tanh(GELU_A * (n + GELU_B * n * n * n))
    slope = 0.5 * (1.0 + t) + 0.5 * n * (1.0 - t * t) * (GELU_A * (1.0 + 3.0 * GELU_B * n * n))
    dn = dhid * slope * pillar_gain[...]
    dbefore[...] = norm_back(b, inverse, dn).astype(BF16)


def latent_kernel(own, other, grad_own, grad_other, out):
    part = dot(own[1], grad_own[...]) + dot(other[1], grad_other[...])
    out[...] = part.astype(BF16)


def pillar_kernel(own, other, grad_own, grad_other, latent, out):
    part = dot(own[0], grad_own[...]) + dot(other[0], grad_other[...])
    out[:, 0] = part.reshape(64, 8, D).astype(BF16)
    out[:, 1] = latent[...].reshape(64, 8, D)


def total_kernel(parts, pillar, latent):
    for k, out in ((0, pillar), (1, latent)):
        out[...] = jnp.sum(parts[:, k].astype(F32), axis=0)


def struct(shape, dtype):
    return jax.ShapeDtypeStruct(shape, dtype)


def call(kernel, name, outs, in_specs, args, scratch=(), flops=0, bytes_accessed=0, limit=28 << 20, out_specs=None):
    many = isinstance(outs, tuple)
    return pl.pallas_call(
        kernel,
        out_shape=outs,
        in_specs=in_specs,
        out_specs=out_specs or (tuple(VMEM for _ in outs) if many else VMEM),
        scratch_shapes=list(scratch),
        name=name,
        cost_estimate=pl.CostEstimate(
            flops=flops, bytes_accessed=bytes_accessed, transcendentals=0
        ),
        compiler_params=pltpu.CompilerParams(vmem_limit_bytes=limit),
    )(*args)


UNIT = 2 * TOK * D * D
MIB = 1 << 20
FRONT_LIMIT = 52 * MIB
TIME_LIMIT = 28 * MIB


def shards(
    counts,
    valid_frames,
    cotangent,
    pillar_proj,
    pillar_gain,
    latent_proj,
    input_proj,
    space_gain,
    space_project,
    space_output,
    time_gain,
    time_project,
    time_output,
):
    rows = struct((TOK, D), BF16)
    scene = ("z", "core", "grp")
    swap = ((0, 1), (1, 0))
    pillar_gain = pillar_gain.reshape(1, D)
    space_gain = space_gain.reshape(1, D)
    time_gain = time_gain.reshape(1, D)

    def exchange(values, axes):
        return lax.all_to_all(values, axes, split_axis=0, concat_axis=0, tiled=True)

    half = struct((2, 512, TOK), BF16)
    wide = lambda n, dtype=BF16: pltpu.VMEM((D, n * D), dtype)
    tall = lambda n, dtype=BF16: pltpu.VMEM((TOK, n * D), dtype)
    own, send, before, stream, joined, packed = call(
        front_kernel,
        "front",
        (half, half, struct((TOK, D), F32), rows, struct((TOK, 3 * D), BF16),
         struct((16, 2, 16, D), BF16)),
        [HBM, HBM, HBM, VMEM, HBM, HBM, VMEM, HBM, HBM],
        (
            counts.reshape(TOK, D), cotangent.reshape(2, 16, 16, D), pillar_proj, pillar_gain,
            latent_proj, input_proj, space_gain, space_project, space_output,
        ),
        [wide(1), wide(1), wide(1), wide(3), wide(1), tall(1, jnp.int32), tall(1),
         pltpu.VMEM((2, 2, 512, TOK), BF16), tall(1, F32), tall(1), tall(3),
         pltpu.SemaphoreType.DMA((9,)), pltpu.SemaphoreType.DMA((5,))],
        8 * UNIT,
        20 * MIB,
        FRONT_LIMIT,
        [HBM, HBM, HBM, HBM, HBM, VMEM],
    )
    packed = exchange(packed, scene)
    grad_tok = call(
        time_kernel,
        "time",
        rows,
        [SMEM, VMEM, VMEM, VMEM, VMEM],
        (valid_frames, packed, time_gain, time_project, time_output),
        [tall(3), tall(1), tall(3), pltpu.VMEM((TOK, TOK), F32)],
        9 * UNIT,
        10 * MIB,
        TIME_LIMIT,
    )
    dspaced = exchange(grad_tok, scene)
    dlatent = call(
        back_kernel,
        "back",
        rows,
        [VMEM] * 7,
        (dspaced, joined, stream, space_gain, space_output, space_project, input_proj),
        [tall(1), tall(3)],
        7 * UNIT,
        14 * MIB,
    )
    dlatent, send = lax.optimization_barrier((dlatent, send))
    other = lax.ppermute(send, "core", swap)
    dlatent_other = lax.ppermute(dlatent, "core", swap)
    dbefore = call(
        token_kernel,
        "token",
        rows,
        [VMEM, VMEM, VMEM, VMEM],
        (dlatent, before, pillar_gain, latent_proj),
        (),
        UNIT,
        4 * MIB,
    )
    dbefore_other = lax.ppermute(dbefore, "core", swap)
    latent_part = call(
        latent_kernel, "latent_weight", struct((512, D), BF16), [VMEM] * 4,
        (own, other, dlatent, dlatent_other), (), UNIT, 2 * MIB,
    )
    parts = call(
        pillar_kernel, "pillar_weight", struct((64, 2, 8, D), BF16), [VMEM] * 5,
        (own, other, dbefore, dbefore_other, latent_part), (), UNIT, 4 * MIB,
    )
    parts = exchange(parts, ("grp", "x", "z", "dp"))
    out = struct((8, D), F32)
    return call(total_kernel, "total", (out, out), [VMEM], (parts,), (), 0, 2 * MIB)


def solution(mesh):
    split = Mesh(mesh.devices.reshape(2, 4, 4, 2, 2), ("grp", "x", "z", "core", "dp"))
    seq = ("x", "z", "core")
    placed = (P("dp", seq, "grp", None, None), P(), P("dp", seq, None, None)) + (P(),) * 10
    out = P(("grp", "x", "z", "core", "dp"), None)
    return jax.shard_map(
        shards, mesh=split, in_specs=placed, out_specs=(out, out), check_vma=False
    )
```

```python
import jax
import jax.numpy as jnp
from jax import lax
from jax.experimental import pallas as pl
from jax.experimental.pallas import tpu as pltpu
from jax.sharding import Mesh, PartitionSpec as P

HEADS = 8
HEAD = 128
FRAMES = 16
TOK = 256
D = 1024
EPS = 1e-06
F32 = jnp.float32
BF16 = jnp.bfloat16
SCALE = HEAD**-0.5
SCALE_LOG2E = SCALE * 1.4426950408889634
VMEM = pl.BlockSpec(memory_space=pltpu.VMEM)
SMEM = pl.BlockSpec(memory_space=pltpu.SMEM)
HBM = pl.BlockSpec(memory_space=pltpu.HBM)


def dot(a, b):
    return lax.dot_general(a, b, (((1,), (0,)), ((), ())), preferred_element_type=F32)


def dot_nt(a, b):
    return lax.dot_general(a, b, (((1,), (1,)), ((), ())), preferred_element_type=F32)


def dot_tn(a, b):
    return lax.dot_general(a, b, (((0,), (0,)), ((), ())), preferred_element_type=F32)


def inverse_rms(values):
    return lax.rsqrt(jnp.mean(values * values, axis=-1, keepdims=True) + EPS)


def norm_back(values, inverse, grad):
    inner = jnp.mean(values * grad, axis=-1, keepdims=True)
    return inverse * grad - values * (inverse * inverse * inverse * inner)


GELU_A = 0.7978845608028654
GELU_B = 0.044715


def head_parts(j_ref, h):
    q = j_ref[:, pl.ds(pl.multiple_of(h * HEAD, HEAD), HEAD)].astype(F32)
    k = j_ref[:, pl.ds(pl.multiple_of(D + h * HEAD, HEAD), HEAD)].astype(F32)
    v = j_ref[:, pl.ds(pl.multiple_of(2 * D + h * HEAD, HEAD), HEAD)]
    iq = inverse_rms(q)
    ik = inverse_rms(k)
    return q, k, v, iq, ik, (q * iq).astype(BF16), (k * ik).astype(BF16)


def softmax(qn, kn, mask):
    w = jnp.exp2(dot_nt(qn, kn) * SCALE_LOG2E)
    if mask is not None:
        w = w * mask
    return w * (1.0 / jnp.sum(w, axis=-1, keepdims=True))


def attention_back(j_ref, dm_ref, dj_ref, mask, h):
    q, k, v, iq, ik, qn, kn = head_parts(j_ref, h)
    weights = softmax(qn, kn, mask)
    cols = pl.ds(pl.multiple_of(h * HEAD, HEAD), HEAD)
    dm = dm_ref[:, cols]
    dp = dot_nt(dm, v).astype(BF16).astype(F32)
    dv = dot_tn(weights.astype(BF16), dm)
    ds = weights * (dp - jnp.sum(dp * weights, axis=-1, keepdims=True))
    ds = ds.astype(BF16)
    dqn = (dot(ds, kn) * SCALE).astype(BF16).astype(F32)
    dkn = (dot_tn(ds, qn) * SCALE).astype(BF16).astype(F32)
    dj_ref[:, cols] = norm_back(q, iq, dqn).astype(BF16)
    dj_ref[:, pl.ds(pl.multiple_of(D + h * HEAD, HEAD), HEAD)] = norm_back(k, ik, dkn).astype(BF16)
    dj_ref[:, pl.ds(pl.multiple_of(2 * D + h * HEAD, HEAD), HEAD)] = dv.astype(BF16)


def front_kernel(
    counts, cotangent, pillar_proj, gains, latent_proj, input_proj, space_project,
    space_output, own, send, before, stream, joined, packed,
    w_pillar, w_latent, w_input, w_project, w_output, counted, mixed,
    v_turned, v_before, v_stream, v_joined, sems, out_sems,
):
    core = lax.axis_index("core")
    copies = [
        pltpu.make_async_copy(src, dst, sems.at[k])
        for k, (src, dst) in enumerate(
            (
                (counts, counted),
                (pillar_proj, w_pillar),
                (latent_proj, w_latent),
                (input_proj, w_input),
                (space_project.at[:, pl.ds(0, D)], w_project.at[:, pl.ds(0, D)]),
                (space_output, w_output),
                (cotangent.at[lax.axis_index("grp")], packed.at[:, 1]),
                (space_project.at[:, pl.ds(D, D)], w_project.at[:, pl.ds(D, D)]),
                (space_project.at[:, pl.ds(2 * D, D)], w_project.at[:, pl.ds(2 * D, D)]),
            )
        )
    ]
    saves = [
        pltpu.make_async_copy(src, dst, out_sems.at[k])
        for k, (src, dst) in enumerate(
            (
                (v_turned.at[:, core], own),
                (v_turned.at[:, 1 - core], send),
                (v_before, before),
                (v_stream, stream),
                (v_joined, joined),
            )
        )
    ]

    def turn(values, k):
        blocks = values.T.reshape(32, 2, 16, TOK)
        v_turned[k, 0] = blocks[:, 0].reshape(512, TOK)
        v_turned[k, 1] = blocks[:, 1].reshape(512, TOK)

    for k in (0, 1, 2, 3, 4, 7, 8, 5, 6):
        copies[k].start()
    copies[0].wait()
    x = jnp.log(counted[...].astype(F32) + 1.0).astype(BF16)
    copies[1].wait()
    b = dot(x, w_pillar[...])
    turn(x, 0)
    v_before[...] = b
    saves[2].start()
    n = b * inverse_rms(b) * gains[0:1]
    hid = (0.5 * n * (1.0 + jnp.tanh(GELU_A * (n + GELU_B * n * n * n)))).astype(BF16)
    copies[2].wait()
    lat = dot(hid, w_latent[...]).astype(BF16)
    turn(hid, 1)
    saves[0].start()
    saves[1].start()
    copies[3].wait()
    s = dot(lat, w_input[...]).astype(BF16)
    v_stream[...] = s
    saves[3].start()
    s = s.astype(F32)
    u = (s * inverse_rms(s) * gains[1:2]).astype(BF16)
    for part, k in enumerate((4, 7, 8)):
        copies[k].wait()
        cols = slice(part * D, (part + 1) * D)
        v_joined[:, cols] = dot(u, w_project[:, cols]).astype(BF16)
    saves[4].start()

    def head(h, carry):
        q, k, v, iq, ik, qn, kn = head_parts(v_joined, h)
        weights = softmax(qn, kn, None).astype(BF16)
        mixed[:, pl.ds(pl.multiple_of(h * HEAD, HEAD), HEAD)] = dot(weights, v).astype(BF16)
        return carry

    lax.fori_loop(0, HEADS, head, 0, unroll=True)
    copies[5].wait()
    spaced = (v_stream[...].astype(F32) + dot(mixed[...], w_output[...])).astype(BF16)
    packed[:, 0] = spaced.reshape(16, 16, D)
    copies[6].wait()
    for save in saves:
        save.wait()


def time_kernel(
    valid_frames, packed, gains, w_project, w_output, grad, joined, dmixed, djoined, masked
):
    valid = valid_frames[lax.axis_index("dp"), lax.axis_index("x")]
    row = lax.broadcasted_iota(jnp.int32, (TOK, TOK), 0)
    col = lax.broadcasted_iota(jnp.int32, (TOK, TOK), 1)
    e = col // FRAMES
    seen = (row % FRAMES == col % FRAMES) & (e <= row // FRAMES) & (e < valid)
    masked[...] = seen.astype(F32)
    s = packed[:, 0].reshape(TOK, D).astype(F32)
    inverse = inverse_rms(s)
    u = (s * inverse * gains[2:3]).astype(BF16)
    for part in range(3):
        cols = slice(part * D, (part + 1) * D)
        joined[:, cols] = dot(u, w_project[:, cols]).astype(BF16)
    dmixed[...] = dot_nt(packed[:, 1].reshape(TOK, D), w_output[...]).astype(BF16)

    def head(h, carry):
        attention_back(joined, dmixed, djoined, masked[...], h)
        return carry

    lax.fori_loop(0, HEADS, head, 0, unroll=True)
    du = dot_nt(djoined[...], w_project[...]).astype(BF16).astype(F32) * gains[2:3]
    s = packed[:, 0].reshape(TOK, D).astype(F32)
    cot = packed[:, 1].reshape(TOK, D).astype(F32)
    grad[...] = (cot + norm_back(s, inverse_rms(s), du)).astype(BF16)


def back_kernel(
    dspaced, joined, stream, gains, w_output, w_project, w_input, dlatent, dmixed, djoined
):
    dmixed[...] = dot_nt(dspaced[...], w_output[...]).astype(BF16)

    def head(h, carry):
        attention_back(joined, dmixed, djoined, None, h)
        return carry

    lax.fori_loop(0, HEADS, head, 0, unroll=True)
    du = dot_nt(djoined[...], w_project[...]).astype(BF16).astype(F32) * gains[1:2]
    s = stream[...].astype(F32)
    dstream = (dspaced[...].astype(F32) + norm_back(s, inverse_rms(s), du)).astype(BF16)
    dlatent[...] = dot_nt(dstream, w_input[...]).astype(BF16)


def token_kernel(dlatent, before, gains, latent_proj, dbefore):
    dhid = dot_nt(dlatent[...], latent_proj[...])
    b = before[...]
    inverse = inverse_rms(b)
    n = b * inverse * gains[0:1]
    t = jnp.tanh(GELU_A * (n + GELU_B * n * n * n))
    slope = 0.5 * (1.0 + t) + 0.5 * n * (1.0 - t * t) * (GELU_A * (1.0 + 3.0 * GELU_B * n * n))
    dn = dhid * slope * gains[0:1]
    dbefore[...] = norm_back(b, inverse, dn).astype(BF16)


def latent_kernel(own, other, grad_own, grad_other, out):
    part = dot(own[1], grad_own[...]) + dot(other[1], grad_other[...])
    out[...] = part.astype(BF16)


def pillar_kernel(own, other, grad_own, grad_other, latent, out):
    part = dot(own[0], grad_own[...]) + dot(other[0], grad_other[...])
    out[:, 0] = part.reshape(64, 8, D).astype(BF16)
    out[:, 1] = latent[...].reshape(64, 8, D)


def total_kernel(parts, pillar, latent):
    for k, out in ((0, pillar), (1, latent)):
        out[...] = jnp.sum(parts[:, k].astype(F32), axis=0)


def struct(shape, dtype):
    return jax.ShapeDtypeStruct(shape, dtype)


def call(kernel, name, outs, in_specs, args, scratch=(), flops=0, bytes_accessed=0, limit=28 << 20, out_specs=None):
    many = isinstance(outs, tuple)
    return pl.pallas_call(
        kernel,
        out_shape=outs,
        in_specs=in_specs,
        out_specs=out_specs or (tuple(VMEM for _ in outs) if many else VMEM),
        scratch_shapes=list(scratch),
        name=name,
        cost_estimate=pl.CostEstimate(
            flops=flops, bytes_accessed=bytes_accessed, transcendentals=0
        ),
        compiler_params=pltpu.CompilerParams(vmem_limit_bytes=limit),
    )(*args)


UNIT = 2 * TOK * D * D
MIB = 1 << 20
FRONT_LIMIT = 52 * MIB
TIME_LIMIT = 28 * MIB


def shards(
    counts,
    valid_frames,
    cotangent,
    pillar_proj,
    pillar_gain,
    latent_proj,
    input_proj,
    space_gain,
    space_project,
    space_output,
    time_gain,
    time_project,
    time_output,
):
    rows = struct((TOK, D), BF16)
    scene = ("z", "core", "grp")
    swap = ((0, 1), (1, 0))
    gains = jnp.stack([pillar_gain, space_gain, time_gain])

    def exchange(values, axes):
        return lax.all_to_all(values, axes, split_axis=0, concat_axis=0, tiled=True)

    half = struct((2, 512, TOK), BF16)
    wide = lambda n, dtype=BF16: pltpu.VMEM((D, n * D), dtype)
    tall = lambda n, dtype=BF16: pltpu.VMEM((TOK, n * D), dtype)
    own, send, before, stream, joined, packed = call(
        front_kernel,
        "front",
        (half, half, struct((TOK, D), F32), rows, struct((TOK, 3 * D), BF16),
         struct((16, 2, 16, D), BF16)),
        [HBM, HBM, HBM, VMEM, HBM, HBM, HBM, HBM],
        (
            counts.reshape(TOK, D), cotangent.reshape(2, 16, 16, D), pillar_proj, gains,
            latent_proj, input_proj, space_project, space_output,
        ),
        [wide(1), wide(1), wide(1), wide(3), wide(1), tall(1, jnp.int32), tall(1),
         pltpu.VMEM((2, 2, 512, TOK), BF16), tall(1, F32), tall(1), tall(3),
         pltpu.SemaphoreType.DMA((9,)), pltpu.SemaphoreType.DMA((5,))],
        8 * UNIT,
        20 * MIB,
        FRONT_LIMIT,
        [HBM, HBM, HBM, HBM, HBM, VMEM],
    )
    packed = exchange(packed, scene)
    grad_tok = call(
        time_kernel,
        "time",
        rows,
        [SMEM, VMEM, VMEM, VMEM, VMEM],
        (valid_frames, packed, gains, time_project, time_output),
        [tall(3), tall(1), tall(3), pltpu.VMEM((TOK, TOK), F32)],
        9 * UNIT,
        10 * MIB,
        TIME_LIMIT,
    )
    dspaced = exchange(grad_tok, scene)
    dlatent = call(
        back_kernel,
        "back",
        rows,
        [VMEM] * 7,
        (dspaced, joined, stream, gains, space_output, space_project, input_proj),
        [tall(1), tall(3)],
        7 * UNIT,
        14 * MIB,
    )
    dlatent, send = lax.optimization_barrier((dlatent, send))
    other = lax.ppermute(send, "core", swap)
    dlatent_other = lax.ppermute(dlatent, "core", swap)
    dbefore = call(
        token_kernel,
        "token",
        rows,
        [VMEM, VMEM, VMEM, VMEM],
        (dlatent, before, gains, latent_proj),
        (),
        UNIT,
        4 * MIB,
    )
    dbefore_other = lax.ppermute(dbefore, "core", swap)
    latent_part = call(
        latent_kernel, "latent_weight", struct((512, D), BF16), [VMEM] * 4,
        (own, other, dlatent, dlatent_other), (), UNIT, 2 * MIB,
    )
    parts = call(
        pillar_kernel, "pillar_weight", struct((64, 2, 8, D), BF16), [VMEM] * 5,
        (own, other, dbefore, dbefore_other, latent_part), (), UNIT, 4 * MIB,
    )
    parts = exchange(parts, ("grp", "x", "z", "dp"))
    out = struct((8, D), F32)
    return call(total_kernel, "total", (out, out), [VMEM], (parts,), (), 0, 2 * MIB)


def solution(mesh):
    split = Mesh(mesh.devices.reshape(2, 4, 4, 2, 2), ("grp", "x", "z", "core", "dp"))
    seq = ("x", "z", "core")
    placed = (P("dp", seq, "grp", None, None), P(), P("dp", seq, None, None)) + (P(),) * 10
    out = P(("grp", "x", "z", "core", "dp"), None)
    return jax.shard_map(
        shards, mesh=split, in_specs=placed, out_specs=(out, out), check_vma=False
    )
```

```python
import jax
import jax.numpy as jnp
from jax import lax
from jax.experimental import pallas as pl
from jax.experimental.pallas import tpu as pltpu
from jax.sharding import Mesh, PartitionSpec as P

HEADS = 8
HEAD = 128
FRAMES = 16
TOK = 256
D = 1024
EPS = 1e-06
F32 = jnp.float32
BF16 = jnp.bfloat16
SCALE = HEAD**-0.5
SCALE_LOG2E = SCALE * 1.4426950408889634
VMEM = pl.BlockSpec(memory_space=pltpu.VMEM)
SMEM = pl.BlockSpec(memory_space=pltpu.SMEM)
HBM = pl.BlockSpec(memory_space=pltpu.HBM)


def dot(a, b):
    return lax.dot_general(a, b, (((1,), (0,)), ((), ())), preferred_element_type=F32)


def dot_nt(a, b):
    return lax.dot_general(a, b, (((1,), (1,)), ((), ())), preferred_element_type=F32)


def dot_tn(a, b):
    return lax.dot_general(a, b, (((0,), (0,)), ((), ())), preferred_element_type=F32)


def inverse_rms(values):
    return lax.rsqrt(jnp.mean(values * values, axis=-1, keepdims=True) + EPS)


def norm_back(values, inverse, grad):
    inner = jnp.mean(values * grad, axis=-1, keepdims=True)
    return inverse * grad - values * (inverse * inverse * inverse * inner)


GELU_A = 0.7978845608028654
GELU_B = 0.044715


def head_parts(j_ref, h):
    q = j_ref[:, pl.ds(pl.multiple_of(h * HEAD, HEAD), HEAD)].astype(F32)
    k = j_ref[:, pl.ds(pl.multiple_of(D + h * HEAD, HEAD), HEAD)].astype(F32)
    v = j_ref[:, pl.ds(pl.multiple_of(2 * D + h * HEAD, HEAD), HEAD)]
    iq = inverse_rms(q)
    ik = inverse_rms(k)
    return q, k, v, iq, ik, (q * iq).astype(BF16), (k * ik).astype(BF16)


def softmax(qn, kn, mask):
    w = jnp.exp2(dot_nt(qn, kn) * SCALE_LOG2E)
    if mask is not None:
        w = w * mask
    return w * (1.0 / jnp.sum(w, axis=-1, keepdims=True))


def attention_back(j_ref, dm_ref, dj_ref, mask, h):
    q, k, v, iq, ik, qn, kn = head_parts(j_ref, h)
    weights = softmax(qn, kn, mask)
    cols = pl.ds(pl.multiple_of(h * HEAD, HEAD), HEAD)
    dm = dm_ref[:, cols]
    dp = dot_nt(dm, v).astype(BF16).astype(F32)
    dv = dot_tn(weights.astype(BF16), dm)
    ds = weights * (dp - jnp.sum(dp * weights, axis=-1, keepdims=True))
    ds = ds.astype(BF16)
    dqn = (dot(ds, kn) * SCALE).astype(BF16).astype(F32)
    dkn = (dot_tn(ds, qn) * SCALE).astype(BF16).astype(F32)
    dj_ref[:, cols] = norm_back(q, iq, dqn).astype(BF16)
    dj_ref[:, pl.ds(pl.multiple_of(D + h * HEAD, HEAD), HEAD)] = norm_back(k, ik, dkn).astype(BF16)
    dj_ref[:, pl.ds(pl.multiple_of(2 * D + h * HEAD, HEAD), HEAD)] = dv.astype(BF16)


def front_kernel(
    counts, cotangent, pillar_proj, gains, latent_proj, input_proj, space_project,
    space_output, own, send, before, stream, joined, packed,
    w_pillar, w_latent, w_input, w_project, w_output, counted, mixed,
    v_turned, v_before, v_stream, v_joined, sems, out_sems,
):
    core = lax.axis_index("core")
    copies = [
        pltpu.make_async_copy(src, dst, sems.at[k])
        for k, (src, dst) in enumerate(
            (
                (counts, counted),
                (pillar_proj, w_pillar),
                (latent_proj, w_latent),
                (input_proj, w_input),
                (space_project.at[:, pl.ds(0, D)], w_project.at[:, pl.ds(0, D)]),
                (space_output, w_output),
                (cotangent.at[lax.axis_index("grp")], packed.at[:, 1]),
                (space_project.at[:, pl.ds(D, D)], w_project.at[:, pl.ds(D, D)]),
                (space_project.at[:, pl.ds(2 * D, D)], w_project.at[:, pl.ds(2 * D, D)]),
            )
        )
    ]
    saves = [
        pltpu.make_async_copy(src, dst, out_sems.at[k])
        for k, (src, dst) in enumerate(
            (
                (v_turned.at[:, core], own),
                (v_turned.at[:, 1 - core], send),
                (v_before, before),
                (v_stream, stream),
                (v_joined, joined),
            )
        )
    ]

    def turn(values, k):
        blocks = values.T.reshape(32, 2, 16, TOK)
        v_turned[k, 0] = blocks[:, 0].reshape(512, TOK)
        v_turned[k, 1] = blocks[:, 1].reshape(512, TOK)

    for k in (0, 1, 2, 3, 4, 7, 8, 5, 6):
        copies[k].start()
    copies[0].wait()
    x = jnp.log(counted[...].astype(F32) + 1.0).astype(BF16)
    copies[1].wait()
    b = dot(x, w_pillar[...])
    turn(x, 0)
    v_before[...] = b
    saves[2].start()
    n = b * inverse_rms(b) * gains[0:1]
    hid = (0.5 * n * (1.0 + jnp.tanh(GELU_A * (n + GELU_B * n * n * n)))).astype(BF16)
    copies[2].wait()
    lat = dot(hid, w_latent[...]).astype(BF16)
    turn(hid, 1)
    saves[0].start()
    saves[1].start()
    copies[3].wait()
    s = dot(lat, w_input[...]).astype(BF16)
    v_stream[...] = s
    saves[3].start()
    s = s.astype(F32)
    u = (s * inverse_rms(s) * gains[1:2]).astype(BF16)
    for part, k in enumerate((4, 7, 8)):
        copies[k].wait()
        cols = slice(part * D, (part + 1) * D)
        v_joined[:, cols] = dot(u, w_project[:, cols]).astype(BF16)
    saves[4].start()

    def head(h, carry):
        q, k, v, iq, ik, qn, kn = head_parts(v_joined, h)
        weights = softmax(qn, kn, None).astype(BF16)
        mixed[:, pl.ds(pl.multiple_of(h * HEAD, HEAD), HEAD)] = dot(weights, v).astype(BF16)
        return carry

    lax.fori_loop(0, HEADS, head, 0, unroll=True)
    copies[5].wait()
    spaced = (v_stream[...].astype(F32) + dot(mixed[...], w_output[...])).astype(BF16)
    packed[:, 0] = spaced.reshape(16, 16, D)
    copies[6].wait()
    for save in saves:
        save.wait()


def time_kernel(
    valid_frames, packed, gains, w_project, w_output, grad, joined, dmixed, djoined, masked
):
    valid = valid_frames[lax.axis_index("dp"), lax.axis_index("x")]
    row = lax.broadcasted_iota(jnp.int32, (TOK, TOK), 0)
    col = lax.broadcasted_iota(jnp.int32, (TOK, TOK), 1)
    e = col // FRAMES
    seen = (row % FRAMES == col % FRAMES) & (e <= row // FRAMES) & (e < valid)
    masked[...] = seen.astype(F32)
    s = packed[:, 0].reshape(TOK, D).astype(F32)
    inverse = inverse_rms(s)
    u = (s * inverse * gains[2:3]).astype(BF16)
    for part in range(3):
        cols = slice(part * D, (part + 1) * D)
        joined[:, cols] = dot(u, w_project[:, cols]).astype(BF16)
    dmixed[...] = dot_nt(packed[:, 1].reshape(TOK, D), w_output[...]).astype(BF16)

    def head(h, carry):
        attention_back(joined, dmixed, djoined, masked[...], h)
        return carry

    lax.fori_loop(0, HEADS, head, 0, unroll=True)
    du = dot_nt(djoined[...], w_project[...]).astype(BF16).astype(F32) * gains[2:3]
    s = packed[:, 0].reshape(TOK, D).astype(F32)
    cot = packed[:, 1].reshape(TOK, D).astype(F32)
    grad[...] = (cot + norm_back(s, inverse_rms(s), du)).astype(BF16)


def back_kernel(
    dspaced, joined, stream, gains, w_output, w_project, w_input, dlatent, dmixed, djoined
):
    dmixed[...] = dot_nt(dspaced[...], w_output[...]).astype(BF16)

    def head(h, carry):
        attention_back(joined, dmixed, djoined, None, h)
        return carry

    lax.fori_loop(0, HEADS, head, 0, unroll=True)
    du = dot_nt(djoined[...], w_project[...]).astype(BF16).astype(F32) * gains[1:2]
    s = stream[...].astype(F32)
    dstream = (dspaced[...].astype(F32) + norm_back(s, inverse_rms(s), du)).astype(BF16)
    dlatent[...] = dot_nt(dstream, w_input[...]).astype(BF16)


def token_kernel(dlatent, before, gains, latent_proj, dbefore):
    dhid = dot_nt(dlatent[...], latent_proj[...])
    b = before[...]
    inverse = inverse_rms(b)
    n = b * inverse * gains[0:1]
    t = jnp.tanh(GELU_A * (n + GELU_B * n * n * n))
    slope = 0.5 * (1.0 + t) + 0.5 * n * (1.0 - t * t) * (GELU_A * (1.0 + 3.0 * GELU_B * n * n))
    dn = dhid * slope * gains[0:1]
    dbefore[...] = norm_back(b, inverse, dn).astype(BF16)


def latent_kernel(own, other, grad_own, grad_other, out):
    part = dot(own[1], grad_own[...]) + dot(other[1], grad_other[...])
    out[...] = part.astype(BF16)


def pillar_kernel(own, other, grad_own, grad_other, latent, out):
    part = dot(own[0], grad_own[...]) + dot(other[0], grad_other[...])
    out[:, 0] = part.reshape(64, 8, D).astype(BF16)
    out[:, 1] = latent[...].reshape(64, 8, D)


def total_kernel(parts, pillar, latent):
    for k, out in ((0, pillar), (1, latent)):
        out[...] = jnp.sum(parts[:, k].astype(F32), axis=0)


def struct(shape, dtype):
    return jax.ShapeDtypeStruct(shape, dtype)


def call(kernel, name, outs, in_specs, args, scratch=(), flops=0, bytes_accessed=0, limit=28 << 20, out_specs=None):
    many = isinstance(outs, tuple)
    return pl.pallas_call(
        kernel,
        out_shape=outs,
        in_specs=in_specs,
        out_specs=out_specs or (tuple(VMEM for _ in outs) if many else VMEM),
        scratch_shapes=list(scratch),
        name=name,
        cost_estimate=pl.CostEstimate(
            flops=flops, bytes_accessed=bytes_accessed, transcendentals=0
        ),
        compiler_params=pltpu.CompilerParams(vmem_limit_bytes=limit),
    )(*args)


UNIT = 2 * TOK * D * D
MIB = 1 << 20
FRONT_LIMIT = 50 * MIB
TIME_LIMIT = 28 * MIB


def shards(
    counts,
    valid_frames,
    cotangent,
    pillar_proj,
    pillar_gain,
    latent_proj,
    input_proj,
    space_gain,
    space_project,
    space_output,
    time_gain,
    time_project,
    time_output,
):
    rows = struct((TOK, D), BF16)
    scene = ("z", "core", "grp")
    swap = ((0, 1), (1, 0))
    gains = jnp.stack([pillar_gain, space_gain, time_gain])

    def exchange(values, axes):
        return lax.all_to_all(values, axes, split_axis=0, concat_axis=0, tiled=True)

    half = struct((2, 512, TOK), BF16)
    wide = lambda n, dtype=BF16: pltpu.VMEM((D, n * D), dtype)
    tall = lambda n, dtype=BF16: pltpu.VMEM((TOK, n * D), dtype)
    own, send, before, stream, joined, packed = call(
        front_kernel,
        "front",
        (half, half, struct((TOK, D), F32), rows, struct((TOK, 3 * D), BF16),
         struct((16, 2, 16, D), BF16)),
        [HBM, HBM, HBM, VMEM, HBM, HBM, HBM, HBM],
        (
            counts.reshape(TOK, D), cotangent.reshape(2, 16, 16, D), pillar_proj, gains,
            latent_proj, input_proj, space_project, space_output,
        ),
        [wide(1), wide(1), wide(1), wide(3), wide(1), tall(1, jnp.int32), tall(1),
         pltpu.VMEM((2, 2, 512, TOK), BF16), tall(1, F32), tall(1), tall(3),
         pltpu.SemaphoreType.DMA((9,)), pltpu.SemaphoreType.DMA((5,))],
        8 * UNIT,
        20 * MIB,
        FRONT_LIMIT,
        [HBM, HBM, HBM, HBM, HBM, VMEM],
    )
    packed = exchange(packed, scene)
    grad_tok = call(
        time_kernel,
        "time",
        rows,
        [SMEM, VMEM, VMEM, VMEM, VMEM],
        (valid_frames, packed, gains, time_project, time_output),
        [tall(3), tall(1), tall(3), pltpu.VMEM((TOK, TOK), F32)],
        9 * UNIT,
        10 * MIB,
        TIME_LIMIT,
    )
    dspaced = exchange(grad_tok, scene)
    dlatent = call(
        back_kernel,
        "back",
        rows,
        [VMEM] * 7,
        (dspaced, joined, stream, gains, space_output, space_project, input_proj),
        [tall(1), tall(3)],
        7 * UNIT,
        14 * MIB,
    )
    dlatent, send = lax.optimization_barrier((dlatent, send))
    other = lax.ppermute(send, "core", swap)
    dlatent_other = lax.ppermute(dlatent, "core", swap)
    dbefore = call(
        token_kernel,
        "token",
        rows,
        [VMEM, VMEM, VMEM, VMEM],
        (dlatent, before, gains, latent_proj),
        (),
        UNIT,
        4 * MIB,
    )
    dbefore_other = lax.ppermute(dbefore, "core", swap)
    latent_part = call(
        latent_kernel, "latent_weight", struct((512, D), BF16), [VMEM] * 4,
        (own, other, dlatent, dlatent_other), (), UNIT, 2 * MIB,
    )
    parts = call(
        pillar_kernel, "pillar_weight", struct((64, 2, 8, D), BF16), [VMEM] * 5,
        (own, other, dbefore, dbefore_other, latent_part), (), UNIT, 4 * MIB,
    )
    parts = exchange(parts, ("grp", "x", "z", "dp"))
    out = struct((8, D), F32)
    return call(total_kernel, "total", (out, out), [VMEM], (parts,), (), 0, 2 * MIB)


def solution(mesh):
    split = Mesh(mesh.devices.reshape(2, 4, 4, 2, 2), ("grp", "x", "z", "core", "dp"))
    seq = ("x", "z", "core")
    placed = (P("dp", seq, "grp", None, None), P(), P("dp", seq, None, None)) + (P(),) * 10
    out = P(("grp", "x", "z", "core", "dp"), None)
    return jax.shard_map(
        shards, mesh=split, in_specs=placed, out_specs=(out, out), check_vma=False
    )
```
